32 devices in a mesh: row: 4 (over y, x), col: 8 (over z, core).
Axes of the slice: x: 2, y: 2, z: 4, core: 2. Of those that a mesh axis runs over, the one named last changes fastest.
Arguments:
- eigvecs: float32 [4096, 4096], P('row', 'col'), may hold values from -6 to 6
- house_one: float32 [4096, 128], P('row', 'col'), may hold values from -0.09375 to 0.09375
- house_two: float32 [4096, 128], P('row', 'col'), may hold values from -0.09375 to 0.09375
- tile_map: int32 [32], replicated, may hold values from 0 to 31, each once
- select: int32 [256], replicated, may hold values from 0 to 4095, as said below
- ritz_basis: bfloat16 [32768, 4096], P(('row', 'col')), may hold values from -0.09375 to 0.09375
Outputs:
- back_vectors: float32 [4096, 4096], P('row', 'col')
- mode_shapes: bfloat16 [32768, 256], P(('row', 'col'))
The draws below stay inside these ranges and needn't reach their ends.
Inputs may be any that keep to these rules, and one draw needn't show every extreme that they name: `select`: the 256 indices are distinct and include 0 and 4095. `tile_map`: each global tile row appears once.
All inputs are finite; a program needn't handle non-finite values.
Results may differ from the reference program's by a relative error of at most 0.0049.
Values may be sent and summed in bfloat16 or wider, within the bound.
No kernel may reach another device: no remote copies, remote signals or barrier semaphores. Data moves between devices by JAX's collectives and lax.ppermute only.
A program may use at most 64 MiB of HBM per device.

```python
import jax
import jax.numpy as jnp
from jax import lax

M = 4096
NB = 128
TILE = 128
P_SIZE = 256
NDOF = 32768


def draw_select(key, part):
    inner = jax.random.permutation(jax.random.fold_in(key, 11), M - 2)[:P_SIZE - 2] + 1
    whole = jnp.concatenate([jnp.array([0, M - 1], jnp.int32), inner.astype(jnp.int32)])
    order = jax.random.permutation(jax.random.fold_in(key, 12), P_SIZE)
    return whole[order]


def block_levels(rng, shape, cuts, smallest, top_value):
    def one(axis_at, parts):
        heights = jax.random.uniform(jax.random.fold_in(jax.random.fold_in(rng, 6), axis_at), (parts,), jnp.float32, smallest / len(cuts), top_value / len(cuts))
        return jnp.repeat(jnp.exp(heights), shape[axis_at] // parts).reshape((-1,) + (1,) * (len(shape) - axis_at - 1))

    gain = one(*cuts[0])
    for cut in cuts[1:]:
        gain = gain * one(*cut)
    return gain


def scatter_about(rng, extent, deviation, limit, shards=(), kind=jnp.bfloat16):
    entries = deviation * jax.random.normal(rng, extent, jnp.float32)
    if shards:
        entries = entries * block_levels(rng, extent, shards, -0.22, 0.18)
    return jnp.clip(entries, -limit, limit).astype(kind)


def setup_inputs(seed: int = 0) -> dict:
    arg_keys = jax.random.split(jax.random.key(seed), 7)
    eigvecs = scatter_about(arg_keys[0], (M, M), 1.0, 6.0, ((0, 4), (1, 8)), jnp.float32)
    house_one = scatter_about(arg_keys[1], (M, NB), M ** -0.5, 0.09375, ((0, 4), (1, 8)), jnp.float32)
    house_two = scatter_about(arg_keys[2], (M, NB), M ** -0.5, 0.09375, ((0, 4), (1, 8)), jnp.float32)
    tile_map = jax.random.permutation(arg_keys[3], M // TILE).astype(jnp.int32)
    select = draw_select(jax.random.fold_in(arg_keys[6], 71), 0)
    ritz_basis = scatter_about(arg_keys[5], (NDOF, M), M ** -0.5, 0.09375, ((0, 32),))
    return {"eigvecs": eigvecs, "house_one": house_one, "house_two": house_two, "tile_map": tile_map, "select": select, "ritz_basis": ritz_basis}


def precise(left, right):
    return jnp.dot(left, right, precision=lax.Precision.HIGHEST, preferred_element_type=jnp.float32)


def compact(gram):
    width = gram.shape[0]
    scales = 0.5 * jnp.diag(gram)
    strict = jnp.triu(gram, 1) / scales[:, None]
    identity = jnp.eye(width, dtype=gram.dtype)
    power = -strict
    total = identity + power
    for level in range((width - 1).bit_length() - 1):
        power = precise(power, power)
        total = precise(total, identity + power)
    return total / scales[None, :]


def reflect(field, vectors):
    factor = compact(precise(vectors.T, vectors))
    return field - precise(vectors, precise(factor, precise(vectors.T, field)))


def reference(eigvecs, house_one, house_two, tile_map, select, ritz_basis):
    section = reflect(eigvecs, house_two)
    back_vectors = reflect(section, house_one)
    panel = back_vectors[:, select].astype(jnp.bfloat16)
    tiles = panel.reshape(M // TILE, TILE, P_SIZE)
    ordered = jnp.zeros_like(tiles).at[tile_map].set(tiles).reshape(M, P_SIZE)
    mode_shapes = jnp.dot(ritz_basis, ordered, preferred_element_type=jnp.float32).astype(jnp.bfloat16)
    return back_vectors, mode_shapes
```

```python
import functools

import jax
import jax.numpy as jnp
from jax import lax
from jax.experimental import pallas as pl
from jax.experimental.pallas import tpu as pltpu
from jax.sharding import PartitionSpec as P

TILE = 128
F32 = jnp.float32
BF16 = jnp.bfloat16


def precise(left, right):
    return jnp.dot(left, right, precision=lax.Precision.HIGHEST, preferred_element_type=F32)


def inverses(grams):
    width = grams[0].shape[0]
    rows = lax.broadcasted_iota(jnp.int32, (width, width), 0)
    cols = lax.broadcasted_iota(jnp.int32, (width, width), 1)
    identity = (rows == cols).astype(F32)
    powers, totals, downs = [], [], []
    for gram in grams:
        diagonal = 0.5 * gram * identity
        across = 1.0 / jnp.sum(diagonal, axis=1, keepdims=True)
        downs.append(1.0 / jnp.sum(diagonal, axis=0, keepdims=True))
        power = jnp.where(rows < cols, -gram * across, 0.0)
        powers.append(power)
        totals.append(identity + power)
    for _ in range((width - 1).bit_length() - 1):
        powers = [precise(power, power) for power in powers]
        totals = [precise(total, identity + power) for total, power in zip(totals, powers)]
    return [total * down for total, down in zip(totals, downs)]


def factor_kernel(place_ref, gram_ref, out_ref):
    size = gram_ref.shape[0]
    half = size // 2
    reflectors = lax.broadcasted_iota(jnp.int32, (size, size), 0)
    order = (reflectors == place_ref[...]).astype(F32)
    turned = (((1,), (1,)), ((), ()))
    gram = lax.dot_general(
        precise(order, gram_ref[...]), order, turned, precision=lax.Precision.HIGHEST, preferred_element_type=F32
    )
    two, one = inverses([gram[:half, :half], gram[half:, half:]])
    mixed = -precise(one, precise(gram[half:, :half], two))
    factor = jnp.concatenate(
        [
            jnp.concatenate([two, jnp.zeros_like(two)], axis=1),
            jnp.concatenate([mixed, one], axis=1),
        ],
        axis=0,
    )
    front = lax.dot_general(
        order, factor, (((0,), (0,)), ((), ())), precision=lax.Precision.HIGHEST, preferred_element_type=F32
    )
    out_ref[...] = precise(front, order)


def factor_of(place, gram):
    size = gram.shape[0]
    return pl.pallas_call(
        factor_kernel,
        out_shape=jax.ShapeDtypeStruct((size, size), F32),
        compiler_params=pltpu.CompilerParams(vmem_limit_bytes=32 << 20),
        cost_estimate=pl.CostEstimate(flops=2 * 6 * 16 * size**3, bytes_accessed=8 * size * size, transcendentals=0),
    )(place, gram)


def modes_kernel(
    here_ref, map_ref, ritz_ref, mine_e, sib_e, mine_v, sib_v, factor_ref, out_ref, sel, vec, buffer, sems
):
    row_at, deep_at, core_at = here_ref[0], here_ref[1], here_ref[2]
    peers, deep, piece, _ = mine_e.shape
    local = mine_v.shape[2]
    chunk = buffer.shape[1]
    steps = ritz_ref.shape[0] // chunk

    def fetch(step):
        return pltpu.make_async_copy(
            ritz_ref.at[pl.ds(step * chunk, chunk)], buffer.at[step], sems.at[step]
        )

    for step in range(steps):
        fetch(step).start()
    tile = min(TILE, local)
    half = vec.shape[0] // 2
    for peer in range(peers):
        start = (row_at ^ peer) * local
        for core, source in ((core_at, mine_e), (1 - core_at, sib_e)):
            for level in range(deep):
                row = start + ((deep_at ^ level) * 2 + core) * piece
                goal = map_ref[row // TILE] * TILE + row % TILE
                sel[pl.ds(pl.multiple_of(goal, piece), piece), :] = source[peer, level]
        for at in range(0, local, tile):
            goal = pl.multiple_of(map_ref[(start + at) // TILE] * TILE, TILE)
            vec[:half, pl.ds(goal, tile)] = mine_v[peer, :, at : at + tile]
            vec[half:, pl.ds(goal, tile)] = sib_v[peer, :, at : at + tile]
    projected = jnp.dot(vec[...], sel[...], preferred_element_type=F32)
    weights = precise(factor_ref[...], projected).astype(BF16)
    change = lax.dot_general(vec[...], weights, (((0,), (0,)), ((), ())), preferred_element_type=F32)
    sel[...] = (sel[...].astype(F32) - change).astype(BF16)
    for step in range(steps):
        fetch(step).wait()
        out_ref[pl.ds(step * chunk, chunk), :] = jnp.dot(
            buffer[step], sel[...], preferred_element_type=F32
        ).astype(BF16)


def modes_of(here, tile_map, ritz_basis, mine_e, sib_e, mine_v, sib_v, factor):
    dofs, order = ritz_basis.shape
    width = mine_e.shape[-1]
    size = factor.shape[0]
    chunk = 256
    in_vmem = pl.BlockSpec(memory_space=pltpu.VMEM)
    in_smem = pl.BlockSpec(memory_space=pltpu.SMEM)
    return pl.pallas_call(
        modes_kernel,
        out_shape=jax.ShapeDtypeStruct((dofs, width), BF16),
        in_specs=[in_smem, in_smem, pl.BlockSpec(memory_space=pl.ANY)] + [in_vmem] * 5,
        out_specs=in_vmem,
        scratch_shapes=[
            pltpu.VMEM((order, width), BF16),
            pltpu.VMEM((size, order), BF16),
            pltpu.VMEM((dofs // chunk, chunk, order), BF16),
            pltpu.SemaphoreType.DMA((dofs // chunk,)),
        ],
        compiler_params=pltpu.CompilerParams(vmem_limit_bytes=48 << 20),
        cost_estimate=pl.CostEstimate(
            flops=2 * order * width * (dofs + 2 * size), bytes_accessed=2 * dofs * order, transcendentals=0
        ),
    )(here, tile_map, ritz_basis, mine_e, sib_e, mine_v, sib_v, factor)


def per_device(rows, cols, eigvecs, house_one, house_two, tile_map, select, ritz_basis):
    deep = cols // 2
    row_at, col_at = lax.axis_index("row"), lax.axis_index("col")
    deep_at, core_at = col_at // 2, col_at % 2
    local, wide = eigvecs.shape
    width = select.shape[0]
    share = house_one.shape[1]
    size = 2 * share * cols

    def to_core(x):
        return lax.ppermute(x, "col", [(i, i ^ 1) for i in range(cols)])

    def to_deep(x, level):
        return lax.ppermute(x, "col", [(i, i ^ (2 * level)) for i in range(cols)])

    def to_row(x, peer):
        return lax.ppermute(x, "row", [(i, i ^ peer) for i in range(rows)])

    own = jnp.concatenate([house_two.T, house_one.T], axis=0).astype(BF16)
    mine_here = jnp.concatenate([own] + [to_deep(own, level) for level in range(1, deep)], axis=0)
    sib_here = to_core(mine_here)
    here_v = jnp.concatenate([mine_here, sib_here], axis=0)
    mine_far = [to_row(mine_here, peer) for peer in range(1, rows)]
    mine_v = jnp.stack([mine_here] + mine_far)
    sib_v = jnp.concatenate([sib_here[None], to_core(jnp.stack(mine_far))])

    field = eigvecs.astype(BF16)
    ids = col_at * wide + jnp.arange(wide, dtype=jnp.int32)
    chooser = (ids[:, None] == select[None, :]).astype(BF16)
    piece = local // cols
    picked = jnp.dot(field, chooser, preferred_element_type=F32).astype(BF16)
    picked = picked.reshape(deep, 2, piece, width)
    first = core_at == 0
    keep = jnp.where(first, picked[:, 0], picked[:, 1])
    give = jnp.where(first, picked[:, 1], picked[:, 0])
    keep = keep + to_core(give)
    block = lax.dynamic_index_in_dim(keep, deep_at, 0, keepdims=False)
    for level in range(1, deep):
        block = block + to_deep(lax.dynamic_index_in_dim(keep, deep_at ^ level, 0, keepdims=False), level)
    mine_sel = jnp.stack([block] + [to_deep(block, level) for level in range(1, deep)])
    mine_e = jnp.stack([mine_sel] + [to_row(mine_sel, peer) for peer in range(1, rows)])
    sib_e = to_core(mine_e)

    part = wide // rows
    partial = jnp.dot(here_v, field, preferred_element_type=F32)

    def chunk_of(x, peer):
        return lax.dynamic_slice_in_dim(x, (row_at ^ peer) * part, part, axis=1)

    projected = chunk_of(partial, 0)
    for peer in range(1, rows):
        projected = projected + to_row(chunk_of(partial, peer).astype(BF16), peer).astype(F32)

    turned = (((1,), (1,)), ((), ()))
    gram = jnp.zeros((size, size), F32)
    for peer in range(rows):
        both = jnp.concatenate([mine_v[peer], sib_v[peer]], axis=0)
        gram = gram + lax.dot_general(both, both, turned, preferred_element_type=F32)
    arrival = jnp.arange(size, dtype=jnp.int32)
    at_share = arrival % share
    at_block = arrival // share % 2
    at_level = arrival // (2 * share) % deep
    at_core = arrival // (2 * share * deep)
    place = at_block * (size // 2) + ((at_level ^ deep_at) * 2 + (at_core ^ core_at)) * share + at_share
    factor = factor_of(place[None, :], gram)

    weights = precise(factor, projected).astype(BF16)
    all_weights = jnp.zeros((size, wide), BF16)
    for peer in range(rows):
        arrived = to_row(weights, peer) if peer else weights
        all_weights = lax.dynamic_update_slice_in_dim(all_weights, arrived, (row_at ^ peer) * part, axis=1)
    change = lax.dot_general(here_v, all_weights, (((0,), (0,)), ((), ())), preferred_element_type=F32)
    back_vectors = eigvecs - change

    here = jnp.stack([row_at, deep_at, core_at]).astype(jnp.int32)
    modes = modes_of(here, tile_map, ritz_basis, mine_e, sib_e, mine_v, sib_v, factor)
    return back_vectors, modes


def solution(mesh):
    return jax.shard_map(
        functools.partial(per_device, mesh.shape["row"], mesh.shape["col"]),
        mesh=mesh,
        in_specs=(P("row", "col"), P("row", "col"), P("row", "col"), P(), P(), P(("row", "col"), None)),
        out_specs=(P("row", "col"), P(("row", "col"), None)),
        check_vma=False,
    )
```

```python
import functools

import jax
import jax.numpy as jnp
from jax import lax
from jax.experimental import pallas as pl
from jax.experimental.pallas import tpu as pltpu
from jax.sharding import PartitionSpec as P

TILE = 128
F32 = jnp.float32
BF16 = jnp.bfloat16


def precise(left, right):
    return jnp.dot(left, right, precision=lax.Precision.HIGHEST, preferred_element_type=F32)


def inverses(grams):
    width = grams[0].shape[0]
    rows = lax.broadcasted_iota(jnp.int32, (width, width), 0)
    cols = lax.broadcasted_iota(jnp.int32, (width, width), 1)
    identity = (rows == cols).astype(F32)
    powers, totals, downs = [], [], []
    for gram in grams:
        diagonal = 0.5 * gram * identity
        across = 1.0 / jnp.sum(diagonal, axis=1, keepdims=True)
        downs.append(1.0 / jnp.sum(diagonal, axis=0, keepdims=True))
        power = jnp.where(rows < cols, -gram * across, 0.0)
        powers.append(power)
        totals.append(identity + power)
    for _ in range((width - 1).bit_length() - 1):
        powers = [precise(power, power) for power in powers]
        totals = [precise(total, identity + power) for total, power in zip(totals, powers)]
    return [total * down for total, down in zip(totals, downs)]


def mirrored(number, rows):
    bits = rows.bit_length() - 1
    return sum(1 << (bits - 1 - bit) for bit in range(bits) if number >> bit & 1)


def pairs_of(mine, sib):
    mine = [part.at[at] for part in mine for at in range(part.shape[0])]
    sib = [part.at[at] for part in sib for at in range(part.shape[0])]
    rows = len(mine)
    for number in range(rows):
        other = mirrored(number, rows)
        yield mine[number], sib[other], (number, other)


def prepare_kernel(
    here_ref, select_ref, eig_ref, two_ref, one_ref, vec_ref, keep_ref, give_ref, buffer, picked, chosen, house, sems
):
    deep_at, core_at = here_ref[1], here_ref[2]
    steps, chunk, wide = buffer.shape
    deep, piece, width = keep_ref.shape
    share = two_ref.shape[0]
    small = [
        pltpu.make_async_copy(select_ref, chosen, sems.at[steps]),
        pltpu.make_async_copy(two_ref, house.at[0], sems.at[steps + 1]),
        pltpu.make_async_copy(one_ref, house.at[1], sems.at[steps + 2]),
    ]
    for copy in small:
        copy.start()

    def fetch(step):
        return pltpu.make_async_copy(eig_ref.at[pl.ds(step * chunk, chunk)], buffer.at[step], sems.at[step])

    for step in range(steps):
        fetch(step).start()
    for copy in small:
        copy.wait()
    vec_ref[:share, :] = house[0].astype(BF16)
    vec_ref[share:, :] = house[1].astype(BF16)
    ids = lax.broadcasted_iota(jnp.int32, (wide, width), 0) + (deep_at * 2 + core_at) * wide
    chooser = jnp.where(ids == chosen[...], 1.0, 0.0).astype(BF16)
    for step in range(steps):
        fetch(step).wait()
        picked[step * chunk : (step + 1) * chunk, :] = jnp.dot(
            buffer[step].astype(BF16), chooser, preferred_element_type=F32
        ).astype(BF16)
    for level in range(deep):
        for out, core in ((keep_ref, core_at), (give_ref, 1 - core_at)):
            row = ((deep_at ^ level) * 2 + core) * piece
            out[level] = picked[pl.ds(pl.multiple_of(row, piece), piece), :]


def prepare(here, select, eigvecs, two, one, cols):
    local, wide = eigvecs.shape
    width = select.shape[0]
    share = two.shape[0]
    deep, piece, steps = cols // 2, local // cols, 4
    in_vmem = pl.BlockSpec(memory_space=pltpu.VMEM)
    some = jax.ShapeDtypeStruct((deep, piece, width), BF16)
    return pl.pallas_call(
        prepare_kernel,
        out_shape=(jax.ShapeDtypeStruct((2 * share, local), BF16), some, some),
        in_specs=[pl.BlockSpec(memory_space=pltpu.SMEM)] + [pl.BlockSpec(memory_space=pltpu.HBM)] * 4,
        out_specs=(in_vmem,) * 3,
        scratch_shapes=[
            pltpu.VMEM((steps, local // steps, wide), F32),
            pltpu.VMEM((local, width), BF16),
            pltpu.VMEM((1, width), jnp.int32),
            pltpu.VMEM((2, share, local), F32),
            pltpu.SemaphoreType.DMA((steps + 3,)),
        ],
        compiler_params=pltpu.CompilerParams(vmem_limit_bytes=16 << 20),
        cost_estimate=pl.CostEstimate(
            flops=2 * local * wide * width, bytes_accessed=4 * local * wide, transcendentals=0
        ),
    )(here, select[None, :], eigvecs, two, one)


def moved(order, x):
    width = x.shape[1]
    high = x.astype(BF16)
    parts = jnp.concatenate([high, (x - high.astype(F32)).astype(BF16)], axis=1)
    both = jnp.dot(order, parts, preferred_element_type=F32)
    return both[:, :width] + both[:, width:]


def factor_kernel(count, place_ref, *refs):
    mine, sib, out_ref = refs[:count], refs[count : 2 * count], refs[2 * count]
    size = out_ref.shape[0]
    half = size // 2
    turned = (((1,), (1,)), ((), ()))
    gram = jnp.zeros((size, size), F32)
    for one, other, _ in pairs_of(mine, sib):
        both = jnp.concatenate([one[...], other[...]], axis=0)
        gram = gram + lax.dot_general(both, both, turned, preferred_element_type=F32)
    reflectors = lax.broadcasted_iota(jnp.int32, (size, size), 0)
    order = jnp.where(reflectors == place_ref[...], 1.0, 0.0)
    back = order.T.astype(BF16)
    order = order.astype(BF16)
    gram = moved(order, moved(order, gram).T)
    two, one = inverses([gram[:half, :half], gram[half:, half:]])
    mixed = -precise(one, precise(gram[half:, :half], two))
    factor = jnp.concatenate(
        [
            jnp.concatenate([two, jnp.zeros_like(two)], axis=1),
            jnp.concatenate([mixed, one], axis=1),
        ],
        axis=0,
    )
    out_ref[...] = moved(back, moved(back, factor).T).T


def factor_of(place, mine, sib):
    _, half, local = mine[0].shape
    size = 2 * half
    rows = sum(part.shape[0] for part in mine)
    return pl.pallas_call(
        functools.partial(factor_kernel, len(mine)),
        out_shape=jax.ShapeDtypeStruct((size, size), F32),
        compiler_params=pltpu.CompilerParams(vmem_limit_bytes=16 << 20),
        cost_estimate=pl.CostEstimate(
            flops=2 * size * size * rows * local + 2 * 6 * 16 * size**3,
            bytes_accessed=8 * size * size + 2 * size * rows * local,
            transcendentals=0,
        ),
    )(place, *mine, *sib)


def spread_kernel(count, here_ref, map_ref, ritz_ref, *refs):
    mine, sib = refs[:count], refs[count : 2 * count]
    vec, out_ref = refs[2 * count :]
    _, half, local = mine[0].shape
    for one, other, numbers in pairs_of(mine, sib):
        start = (here_ref[0] ^ jnp.where(here_ref[2] == 0, *numbers)) * local
        for at in range(0, local, TILE):
            goal = pl.multiple_of(map_ref[(start + at) // TILE] * TILE, TILE)
            vec[:half, pl.ds(goal, TILE)] = one[:, at : at + TILE]
            vec[half:, pl.ds(goal, TILE)] = other[:, at : at + TILE]
    out_ref[...] = lax.dot_general(
        ritz_ref[...], vec[...], (((1,), (1,)), ((), ())), preferred_element_type=F32
    ).astype(BF16)


def spread(here, tile_map, ritz_basis, mine, sib):
    dofs, order = ritz_basis.shape
    size = 2 * mine[0].shape[1]
    in_vmem = pl.BlockSpec(memory_space=pltpu.VMEM)
    in_smem = pl.BlockSpec(memory_space=pltpu.SMEM)
    return pl.pallas_call(
        functools.partial(spread_kernel, len(mine)),
        out_shape=(jax.ShapeDtypeStruct((size, order), BF16), jax.ShapeDtypeStruct((dofs, size), BF16)),
        in_specs=[in_smem, in_smem] + [in_vmem] * (1 + 2 * len(mine)),
        out_specs=(in_vmem, in_vmem),
        compiler_params=pltpu.CompilerParams(vmem_limit_bytes=16 << 20),
        cost_estimate=pl.CostEstimate(
            flops=2 * order * size * dofs, bytes_accessed=2 * dofs * order, transcendentals=0
        ),
    )(here, tile_map, ritz_basis, *mine, *sib)


def modes_kernel(count, here_ref, map_ref, ritz_ref, vec_ref, spread_ref, factor_ref, *refs):
    mine, sib = refs[:count], refs[count : 2 * count]
    out_ref, sel = refs[2 * count :]
    _, deep, piece, _ = mine[0].shape
    local = 2 * deep * piece
    for one, other, numbers in pairs_of(mine, sib):
        start = (here_ref[0] ^ jnp.where(here_ref[2] == 0, *numbers)) * local
        for core, source in ((here_ref[2], one), (1 - here_ref[2], other)):
            for level in range(deep):
                row = start + ((here_ref[1] ^ level) * 2 + core) * piece
                goal = pl.multiple_of(map_ref[row // TILE] * TILE + row % TILE, piece)
                sel[pl.ds(goal, piece), :] = source[level]
    projected = jnp.dot(vec_ref[...], sel[...], preferred_element_type=F32)
    weights = precise(factor_ref[...], projected).astype(BF16)
    modes = jnp.dot(ritz_ref[...], sel[...], preferred_element_type=F32)
    modes = modes - jnp.dot(spread_ref[...], weights, preferred_element_type=F32)
    out_ref[...] = modes.astype(BF16)


def modes_of(here, tile_map, ritz_basis, vec, spreads, factor, mine, sib):
    dofs, order = ritz_basis.shape
    width = mine[0].shape[-1]
    size = factor.shape[0]
    in_vmem = pl.BlockSpec(memory_space=pltpu.VMEM)
    in_smem = pl.BlockSpec(memory_space=pltpu.SMEM)
    return pl.pallas_call(
        functools.partial(modes_kernel, len(mine)),
        out_shape=jax.ShapeDtypeStruct((dofs, width), BF16),
        in_specs=[in_smem, in_smem] + [in_vmem] * (4 + 2 * len(mine)),
        out_specs=in_vmem,
        scratch_shapes=[pltpu.VMEM((order, width), BF16)],
        compiler_params=pltpu.CompilerParams(vmem_limit_bytes=16 << 20),
        cost_estimate=pl.CostEstimate(
            flops=2 * order * width * (dofs + size), bytes_accessed=2 * dofs * order, transcendentals=0
        ),
    )(here, tile_map, ritz_basis, vec, spreads, factor, *mine, *sib)


def per_device(rows, cols, eigvecs, house_one, house_two, tile_map, select, ritz_basis):
    deep = cols // 2
    row_at, col_at = lax.axis_index("row"), lax.axis_index("col")
    deep_at, core_at = col_at // 2, col_at % 2
    here = jnp.stack([row_at, deep_at, core_at]).astype(jnp.int32)
    local, wide = eigvecs.shape
    share = house_one.shape[1]
    size = 2 * share * cols

    def to_core(x):
        return lax.ppermute(x, "col", [(i, i ^ 1) for i in range(cols)])

    def to_deep(x, level):
        return lax.ppermute(x, "col", [(i, i ^ (2 * level)) for i in range(cols)])

    def to_row(x, peer):
        return lax.ppermute(x, "row", [(i, i ^ peer) for i in range(rows)])

    steps = rows.bit_length() - 1

    def over_step(x, step):
        pairs = []
        for row in range(rows):
            for col in range(cols):
                bit = steps - 1 - step if col % 2 else step
                pairs.append((row * cols + col, (row ^ (1 << bit)) * cols + col))
        return lax.ppermute(x, ("row", "col"), pairs)

    def over_rows(x, after=None):
        parts = [x[None]]
        for step in range(steps):
            held = jnp.concatenate(parts) if step else parts[0]
            if after is not None:
                held = lax.optimization_barrier((held, after(step)))[0]
            parts.append(over_step(held, step))
        return parts

    own, keep, give = prepare(here, select, eigvecs, house_two.T, house_one.T, cols)

    got, own = lax.optimization_barrier((to_core(give), own))
    keep = keep + got

    mine_here = jnp.concatenate([own] + [to_deep(own, level) for level in range(1, deep)], axis=0)
    mine_here, keep = lax.optimization_barrier((mine_here, keep))
    mine_v = over_rows(mine_here)
    sib_v = [to_core(x) for x in mine_v]

    part = wide // rows
    here_v = jnp.concatenate([mine_here, sib_v[0][0]], axis=0)
    partial = jnp.dot(here_v, eigvecs.astype(BF16), preferred_element_type=F32)

    def chunk_of(number):
        away = jnp.where(core_at == 0, number, mirrored(number, rows))
        return lax.dynamic_slice_in_dim(partial, (row_at ^ away) * part, part, axis=1)

    chunks = jnp.stack([chunk_of(number) for number in range(rows)])
    block, chunks = lax.optimization_barrier((keep[0], chunks))
    sums = []
    for step in reversed(range(steps)):
        kept = 1 << step
        chunks = chunks[:kept] + over_step(chunks[kept:].astype(BF16), step).astype(F32)
        sums.append(chunks)
    projected = chunks[0]

    arrival = jnp.arange(size, dtype=jnp.int32)
    at_share = arrival % share
    at_block = arrival // share % 2
    at_level = arrival // (2 * share) % deep
    at_core = arrival // (2 * share * deep)
    place = at_block * (size // 2) + ((at_level ^ deep_at) * 2 + (at_core ^ core_at)) * share + at_share
    factor = factor_of(place[None, :], mine_v, sib_v)

    for level in range(1, deep):
        block = block + to_deep(keep[level], level)
    mine_sel = jnp.stack([block] + [to_deep(block, level) for level in range(1, deep)])
    mine_e = over_rows(mine_sel, lambda step: sums[step] if step else (sums[step], sib_v))
    sib_e = [to_core(x) for x in mine_e]

    weights = precise(factor, projected).astype(BF16)
    all_weights = jnp.zeros((size, wide), BF16)
    for peer in range(rows):
        arrived = to_row(weights, peer) if peer else weights
        all_weights = lax.dynamic_update_slice_in_dim(all_weights, arrived, (row_at ^ peer) * part, axis=1)
    change = lax.dot_general(here_v, all_weights, (((0,), (0,)), ((), ())), preferred_element_type=F32)
    back_vectors = eigvecs - change

    vec, spreads = spread(here, tile_map, ritz_basis, mine_v, sib_v)
    modes = modes_of(here, tile_map, ritz_basis, vec, spreads, factor, mine_e, sib_e)
    return back_vectors, modes


def solution(mesh):
    return jax.shard_map(
        functools.partial(per_device, mesh.shape["row"], mesh.shape["col"]),
        mesh=mesh,
        in_specs=(P("row", "col"), P("row", "col"), P("row", "col"), P(), P(), P(("row", "col"), None)),
        out_specs=(P("row", "col"), P(("row", "col"), None)),
        check_vma=False,
    )
```

```python
import functools

import jax
import jax.numpy as jnp
from jax import lax
from jax.experimental import pallas as pl
from jax.experimental.pallas import tpu as pltpu
from jax.sharding import PartitionSpec as P

TILE = 128
F32 = jnp.float32
BF16 = jnp.bfloat16


def precise(left, right):
    return jnp.dot(left, right, precision=lax.Precision.HIGHEST, preferred_element_type=F32)


def inverses(grams):
    width = grams[0].shape[0]
    rows = lax.broadcasted_iota(jnp.int32, (width, width), 0)
    cols = lax.broadcasted_iota(jnp.int32, (width, width), 1)
    identity = (rows == cols).astype(F32)
    powers, totals, downs = [], [], []
    for gram in grams:
        diagonal = 0.5 * gram * identity
        across = 1.0 / jnp.sum(diagonal, axis=1, keepdims=True)
        downs.append(1.0 / jnp.sum(diagonal, axis=0, keepdims=True))
        power = jnp.where(rows < cols, -gram * across, 0.0)
        powers.append(power)
        totals.append(identity + power)
    for _ in range((width - 1).bit_length() - 1):
        powers = [precise(power, power) for power in powers]
        totals = [precise(total, identity + power) for total, power in zip(totals, powers)]
    return [total * down for total, down in zip(totals, downs)]


def mirrored(number, rows):
    bits = rows.bit_length() - 1
    return sum(1 << (bits - 1 - bit) for bit in range(bits) if number >> bit & 1)


def pairs_of(mine, sib):
    mine = [part.at[at] for part in mine for at in range(part.shape[0])]
    sib = [part.at[at] for part in sib for at in range(part.shape[0])]
    rows = len(mine)
    for number in range(rows):
        other = mirrored(number, rows)
        yield mine[number], sib[other], (number, other)


def prepare_kernel(here_ref, select_ref, eig_ref, keep_ref, give_ref, picked):
    deep_at, core_at = here_ref[1], here_ref[2]
    local, wide = eig_ref.shape
    deep, piece, width = keep_ref.shape
    ids = lax.broadcasted_iota(jnp.int32, (wide, width), 0) + (deep_at * 2 + core_at) * wide
    chooser = jnp.where(ids == select_ref[...], 1.0, 0.0).astype(BF16)
    picked[...] = jnp.dot(eig_ref[...].astype(BF16), chooser, preferred_element_type=F32).astype(BF16)
    for level in range(deep):
        for out, core in ((keep_ref, core_at), (give_ref, 1 - core_at)):
            row = ((deep_at ^ level) * 2 + core) * piece
            out[level] = picked[pl.ds(pl.multiple_of(row, piece), piece), :]


def prepare(here, select, eigvecs, cols):
    local, wide = eigvecs.shape
    width = select.shape[0]
    deep, piece = cols // 2, local // cols
    in_vmem = pl.BlockSpec(memory_space=pltpu.VMEM)
    some = jax.ShapeDtypeStruct((deep, piece, width), BF16)
    return pl.pallas_call(
        prepare_kernel,
        out_shape=(some, some),
        in_specs=[pl.BlockSpec(memory_space=pltpu.SMEM), in_vmem, in_vmem],
        out_specs=(in_vmem,) * 2,
        scratch_shapes=[pltpu.VMEM((local, width), BF16)],
        compiler_params=pltpu.CompilerParams(vmem_limit_bytes=16 << 20),
        cost_estimate=pl.CostEstimate(
            flops=2 * local * wide * width, bytes_accessed=4 * local * wide, transcendentals=0
        ),
    )(here, select[None, :], eigvecs)


def moved(order, x):
    width = x.shape[1]
    high = x.astype(BF16)
    parts = jnp.concatenate([high, (x - high.astype(F32)).astype(BF16)], axis=1)
    both = jnp.dot(order, parts, preferred_element_type=F32)
    return both[:, :width] + both[:, width:]


def factor_kernel(count, place_ref, *refs):
    mine, sib, out_ref = refs[:count], refs[count : 2 * count], refs[2 * count]
    size = out_ref.shape[0]
    half = size // 2
    turned = (((1,), (1,)), ((), ()))
    gram = jnp.zeros((size, size), F32)
    for one, other, _ in pairs_of(mine, sib):
        both = jnp.concatenate([one[...], other[...]], axis=0)
        gram = gram + lax.dot_general(both, both, turned, preferred_element_type=F32)
    reflectors = lax.broadcasted_iota(jnp.int32, (size, size), 0)
    order = jnp.where(reflectors == place_ref[...], 1.0, 0.0)
    back = order.T.astype(BF16)
    order = order.astype(BF16)
    gram = moved(order, moved(order, gram).T)
    two, one = inverses([gram[:half, :half], gram[half:, half:]])
    mixed = -precise(one, precise(gram[half:, :half], two))
    factor = jnp.concatenate(
        [
            jnp.concatenate([two, jnp.zeros_like(two)], axis=1),
            jnp.concatenate([mixed, one], axis=1),
        ],
        axis=0,
    )
    out_ref[...] = moved(back, moved(back, factor).T).T


def factor_of(place, mine, sib):
    _, half, local = mine[0].shape
    size = 2 * half
    rows = sum(part.shape[0] for part in mine)
    return pl.pallas_call(
        functools.partial(factor_kernel, len(mine)),
        out_shape=jax.ShapeDtypeStruct((size, size), F32),
        compiler_params=pltpu.CompilerParams(vmem_limit_bytes=16 << 20),
        cost_estimate=pl.CostEstimate(
            flops=2 * size * size * rows * local + 2 * 6 * 16 * size**3,
            bytes_accessed=8 * size * size + 2 * size * rows * local,
            transcendentals=0,
        ),
    )(place, *mine, *sib)


def spread_kernel(count, here_ref, map_ref, ritz_ref, *refs):
    mine, sib = refs[:count], refs[count : 2 * count]
    vec, out_ref = refs[2 * count :]
    _, half, local = mine[0].shape
    for one, other, numbers in pairs_of(mine, sib):
        start = (here_ref[0] ^ jnp.where(here_ref[2] == 0, *numbers)) * local
        for at in range(0, local, TILE):
            goal = pl.multiple_of(map_ref[(start + at) // TILE] * TILE, TILE)
            vec[:half, pl.ds(goal, TILE)] = one[:, at : at + TILE]
            vec[half:, pl.ds(goal, TILE)] = other[:, at : at + TILE]
    out_ref[...] = lax.dot_general(
        ritz_ref[...], vec[...], (((1,), (1,)), ((), ())), preferred_element_type=F32
    ).astype(BF16)


def spread(here, tile_map, ritz_basis, mine, sib):
    dofs, order = ritz_basis.shape
    size = 2 * mine[0].shape[1]
    in_vmem = pl.BlockSpec(memory_space=pltpu.VMEM)
    in_smem = pl.BlockSpec(memory_space=pltpu.SMEM)
    return pl.pallas_call(
        functools.partial(spread_kernel, len(mine)),
        out_shape=(jax.ShapeDtypeStruct((size, order), BF16), jax.ShapeDtypeStruct((dofs, size), BF16)),
        in_specs=[in_smem, in_smem] + [in_vmem] * (1 + 2 * len(mine)),
        out_specs=(in_vmem, in_vmem),
        compiler_params=pltpu.CompilerParams(vmem_limit_bytes=16 << 20),
        cost_estimate=pl.CostEstimate(
            flops=2 * order * size * dofs, bytes_accessed=2 * dofs * order, transcendentals=0
        ),
    )(here, tile_map, ritz_basis, *mine, *sib)


def modes_kernel(count, here_ref, map_ref, ritz_ref, vec_ref, spread_ref, factor_ref, *refs):
    mine, sib = refs[:count], refs[count : 2 * count]
    out_ref, sel = refs[2 * count :]
    _, deep, piece, _ = mine[0].shape
    local = 2 * deep * piece
    for one, other, numbers in pairs_of(mine, sib):
        start = (here_ref[0] ^ jnp.where(here_ref[2] == 0, *numbers)) * local
        for core, source in ((here_ref[2], one), (1 - here_ref[2], other)):
            for level in range(deep):
                row = start + ((here_ref[1] ^ level) * 2 + core) * piece
                goal = pl.multiple_of(map_ref[row // TILE] * TILE + row % TILE, piece)
                sel[pl.ds(goal, piece), :] = source[level]
    projected = jnp.dot(vec_ref[...], sel[...], preferred_element_type=F32)
    weights = precise(factor_ref[...], projected).astype(BF16)
    modes = jnp.dot(ritz_ref[...], sel[...], preferred_element_type=F32)
    modes = modes - jnp.dot(spread_ref[...], weights, preferred_element_type=F32)
    out_ref[...] = modes.astype(BF16)


def modes_of(here, tile_map, ritz_basis, vec, spreads, factor, mine, sib):
    dofs, order = ritz_basis.shape
    width = mine[0].shape[-1]
    size = factor.shape[0]
    in_vmem = pl.BlockSpec(memory_space=pltpu.VMEM)
    in_smem = pl.BlockSpec(memory_space=pltpu.SMEM)
    return pl.pallas_call(
        functools.partial(modes_kernel, len(mine)),
        out_shape=jax.ShapeDtypeStruct((dofs, width), BF16),
        in_specs=[in_smem, in_smem] + [in_vmem] * (4 + 2 * len(mine)),
        out_specs=in_vmem,
        scratch_shapes=[pltpu.VMEM((order, width), BF16)],
        compiler_params=pltpu.CompilerParams(vmem_limit_bytes=16 << 20),
        cost_estimate=pl.CostEstimate(
            flops=2 * order * width * (dofs + size), bytes_accessed=2 * dofs * order, transcendentals=0
        ),
    )(here, tile_map, ritz_basis, vec, spreads, factor, *mine, *sib)


def sort_kernel(count, here_ref, map_ref, ritz_ref, *refs):
    mine, sib = refs[:count], refs[count : 2 * count]
    ritz_out, vec, out_ref = refs[2 * count :]
    _, half, local = mine[0].shape
    deep = local // TILE // 2
    blocks = list(pairs_of(mine, sib))
    rows = len(blocks)
    for one, other, numbers in blocks:
        row = here_ref[0] ^ jnp.where(here_ref[2] == 0, *numbers)
        for level in range(deep):
            for side in (0, 1):
                core = here_ref[2] ^ side
                tile = (here_ref[1] ^ level) * 2 + core
                place = ((side * rows + numbers[side]) * deep + level) * TILE
                to = slice(place, place + TILE)
                goal = pl.multiple_of(map_ref[row * 2 * deep + tile] * TILE, TILE)
                at = pl.multiple_of(tile * TILE, TILE)
                ritz_out[:, to] = ritz_ref[:, pl.ds(goal, TILE)]
                vec[:half, to] = one[:, pl.ds(at, TILE)]
                vec[half:, to] = other[:, pl.ds(at, TILE)]
    out_ref[...] = lax.dot_general(
        ritz_out[...], vec[...], (((1,), (1,)), ((), ())), preferred_element_type=F32
    ).astype(BF16)


def sort(here, tile_map, ritz_basis, mine, sib):
    dofs, order = ritz_basis.shape
    size = 2 * mine[0].shape[1]
    in_vmem = pl.BlockSpec(memory_space=pltpu.VMEM)
    in_smem = pl.BlockSpec(memory_space=pltpu.SMEM)
    return pl.pallas_call(
        functools.partial(sort_kernel, len(mine)),
        out_shape=(
            jax.ShapeDtypeStruct((dofs, order), BF16),
            jax.ShapeDtypeStruct((size, order), BF16),
            jax.ShapeDtypeStruct((dofs, size), BF16),
        ),
        in_specs=[in_smem, in_smem] + [in_vmem] * (1 + 2 * len(mine)),
        out_specs=(in_vmem,) * 3,
        compiler_params=pltpu.CompilerParams(vmem_limit_bytes=24 << 20),
        cost_estimate=pl.CostEstimate(
            flops=2 * order * size * dofs, bytes_accessed=4 * dofs * order, transcendentals=0
        ),
    )(here, tile_map, ritz_basis, *mine, *sib)


def blocks_in(parts):
    return jnp.concatenate([part[...].reshape(-1, part.shape[-1]) for part in parts], axis=0)


def first_kernel(ritz_ref, vec_ref, *refs):
    mine, (modes_ref, projected_ref) = refs[:-2], refs[-2:]
    sel = blocks_in(mine)
    depth = sel.shape[0]
    projected_ref[...] = jnp.dot(vec_ref[:, :depth], sel, preferred_element_type=F32)
    modes_ref[...] = jnp.dot(ritz_ref[:, :depth], sel, preferred_element_type=F32)


def second_kernel(ritz_ref, vec_ref, spread_ref, factor_ref, modes_ref, projected_ref, *refs):
    sib, out_ref = refs[:-1], refs[-1]
    sel = blocks_in(sib)
    depth = sel.shape[0]
    projected = projected_ref[...] + jnp.dot(vec_ref[:, depth:], sel, preferred_element_type=F32)
    weights = precise(factor_ref[...], projected).astype(BF16)
    modes = modes_ref[...] + jnp.dot(ritz_ref[:, depth:], sel, preferred_element_type=F32)
    modes = modes - jnp.dot(spread_ref[...], weights, preferred_element_type=F32)
    out_ref[...] = modes.astype(BF16)


def modes_in_two(ritz_sorted, vec, spreads, factor, mine, sib):
    dofs, order = ritz_sorted.shape
    width = mine[0].shape[-1]
    size = factor.shape[0]
    in_vmem = pl.BlockSpec(memory_space=pltpu.VMEM)
    params = pltpu.CompilerParams(vmem_limit_bytes=16 << 20)
    cost = pl.CostEstimate(
        flops=order * width * (dofs + size), bytes_accessed=dofs * order, transcendentals=0
    )
    modes, projected = pl.pallas_call(
        first_kernel,
        out_shape=(jax.ShapeDtypeStruct((dofs, width), F32), jax.ShapeDtypeStruct((size, width), F32)),
        in_specs=[in_vmem] * (2 + len(mine)),
        out_specs=(in_vmem, in_vmem),
        compiler_params=params,
        cost_estimate=cost,
    )(ritz_sorted, vec, *mine)
    return pl.pallas_call(
        second_kernel,
        out_shape=jax.ShapeDtypeStruct((dofs, width), BF16),
        in_specs=[in_vmem] * (6 + len(sib)),
        out_specs=in_vmem,
        compiler_params=params,
        cost_estimate=cost,
    )(ritz_sorted, vec, spreads, factor, modes, projected, *sib)


def per_device(rows, cols, eigvecs, house_one, house_two, tile_map, select, ritz_basis):
    deep = cols // 2
    row_at, col_at = lax.axis_index("row"), lax.axis_index("col")
    deep_at, core_at = col_at // 2, col_at % 2
    here = jnp.stack([row_at, deep_at, core_at]).astype(jnp.int32)
    local, wide = eigvecs.shape
    share = house_one.shape[1]
    size = 2 * share * cols

    def to_core(x):
        return lax.ppermute(x, "col", [(i, i ^ 1) for i in range(cols)])

    def to_deep(x, level):
        return lax.ppermute(x, "col", [(i, i ^ (2 * level)) for i in range(cols)])

    def to_row(x, peer):
        return lax.ppermute(x, "row", [(i, i ^ peer) for i in range(rows)])

    steps = rows.bit_length() - 1

    def over_step(x, step):
        pairs = []
        for row in range(rows):
            for col in range(cols):
                bit = steps - 1 - step if col % 2 else step
                pairs.append((row * cols + col, (row ^ (1 << bit)) * cols + col))
        return lax.ppermute(x, ("row", "col"), pairs)

    def over_rows(x, after=None):
        parts = [x[None]]
        for step in range(steps):
            held = jnp.concatenate(parts) if step else parts[0]
            if after is not None:
                held = lax.optimization_barrier((held, after(step)))[0]
            parts.append(over_step(held, step))
        return parts

    keep, give = prepare(here, select, eigvecs, cols)
    own = jnp.pad(house_two.T, ((0, share), (0, 0))) + jnp.pad(house_one.T, ((share, 0), (0, 0)))
    own = own.astype(BF16)

    got, own = lax.optimization_barrier((to_core(give), own))
    keep = keep + got

    mine_here = jnp.concatenate([own] + [to_deep(own, level) for level in range(1, deep)], axis=0)
    mine_here, keep = lax.optimization_barrier((mine_here, keep))
    mine_v = over_rows(mine_here)
    sib_v = [to_core(x) for x in mine_v]

    part = wide // rows
    here_v = jnp.concatenate([mine_here, sib_v[0][0]], axis=0)
    partial = jnp.dot(here_v, eigvecs.astype(BF16), preferred_element_type=F32)

    def chunk_of(number):
        away = jnp.where(core_at == 0, number, mirrored(number, rows))
        return lax.dynamic_slice_in_dim(partial, (row_at ^ away) * part, part, axis=1)

    chunks = jnp.stack([chunk_of(number) for number in range(rows)])
    block, chunks = lax.optimization_barrier((keep[0], chunks))
    sums = []
    for step in reversed(range(steps)):
        kept = 1 << step
        chunks = chunks[:kept] + over_step(chunks[kept:].astype(BF16), step).astype(F32)
        sums.append(chunks)
    projected = chunks[0]

    arrival = jnp.arange(size, dtype=jnp.int32)
    at_share = arrival % share
    at_block = arrival // share % 2
    at_level = arrival // (2 * share) % deep
    at_core = arrival // (2 * share * deep)
    place = at_block * (size // 2) + ((at_level ^ deep_at) * 2 + (at_core ^ core_at)) * share + at_share
    factor = factor_of(place[None, :], mine_v, sib_v)

    for level in range(1, deep):
        block = block + to_deep(keep[level], level)
    mine_sel = jnp.stack([block] + [to_deep(block, level) for level in range(1, deep)])
    mine_e = over_rows(mine_sel, lambda step: sums[step] if step else (sums[step], sib_v))
    sib_e = [to_core(x) for x in mine_e]

    weights = precise(factor, projected).astype(BF16)
    all_weights = jnp.zeros((size, wide), BF16)
    for peer in range(rows):
        arrived = to_row(weights, peer) if peer else weights
        all_weights = lax.dynamic_update_slice_in_dim(all_weights, arrived, (row_at ^ peer) * part, axis=1)
    change = lax.dot_general(here_v, all_weights, (((0,), (0,)), ((), ())), preferred_element_type=F32)
    back_vectors = eigvecs - change

    if local // cols == TILE:
        ritz_sorted, vec, spreads = sort(here, tile_map, ritz_basis, mine_v, sib_v)
        modes = modes_in_two(ritz_sorted, vec, spreads, factor, mine_e, sib_e)
    else:
        vec, spreads = spread(here, tile_map, ritz_basis, mine_v, sib_v)
        modes = modes_of(here, tile_map, ritz_basis, vec, spreads, factor, mine_e, sib_e)
    return back_vectors, modes


def solution(mesh):
    return jax.shard_map(
        functools.partial(per_device, mesh.shape["row"], mesh.shape["col"]),
        mesh=mesh,
        in_specs=(P("row", "col"), P("row", "col"), P("row", "col"), P(), P(), P(("row", "col"), None)),
        out_specs=(P("row", "col"), P(("row", "col"), None)),
        check_vma=False,
    )
```

```python
import functools

import jax
import jax.numpy as jnp
from jax import lax
from jax.experimental import pallas as pl
from jax.experimental.pallas import tpu as pltpu
from jax.sharding import PartitionSpec as P

TILE = 128
F32 = jnp.float32
BF16 = jnp.bfloat16


def precise(left, right):
    return jnp.dot(left, right, precision=lax.Precision.HIGHEST, preferred_element_type=F32)


def inverses(grams):
    width = grams[0].shape[0]
    rows = lax.broadcasted_iota(jnp.int32, (width, width), 0)
    cols = lax.broadcasted_iota(jnp.int32, (width, width), 1)
    identity = (rows == cols).astype(F32)
    powers, totals, downs = [], [], []
    for gram in grams:
        diagonal = 0.5 * gram * identity
        across = 1.0 / jnp.sum(diagonal, axis=1, keepdims=True)
        downs.append(1.0 / jnp.sum(diagonal, axis=0, keepdims=True))
        power = jnp.where(rows < cols, -gram * across, 0.0)
        powers.append(power)
        totals.append(identity + power)
    for _ in range((width - 1).bit_length() - 1):
        powers = [precise(power, power) for power in powers]
        totals = [precise(total, identity + power) for total, power in zip(totals, powers)]
    return [total * down for total, down in zip(totals, downs)]


def mirrored(number, rows):
    bits = rows.bit_length() - 1
    return sum(1 << (bits - 1 - bit) for bit in range(bits) if number >> bit & 1)


def pairs_of(mine, sib):
    mine = [part.at[at] for part in mine for at in range(part.shape[0])]
    sib = [part.at[at] for part in sib for at in range(part.shape[0])]
    rows = len(mine)
    for number in range(rows):
        other = mirrored(number, rows)
        yield mine[number], sib[other], (number, other)


def prepare_kernel(here_ref, select_ref, eig_ref, keep_ref, give_ref, picked):
    deep_at, core_at = here_ref[1], here_ref[2]
    local, wide = eig_ref.shape
    deep, piece, width = keep_ref.shape
    ids = lax.broadcasted_iota(jnp.int32, (wide, width), 0) + (deep_at * 2 + core_at) * wide
    chooser = jnp.where(ids == select_ref[...], 1.0, 0.0).astype(BF16)
    picked[...] = jnp.dot(eig_ref[...].astype(BF16), chooser, preferred_element_type=F32).astype(BF16)
    for level in range(deep):
        for out, core in ((keep_ref, core_at), (give_ref, 1 - core_at)):
            row = ((deep_at ^ level) * 2 + core) * piece
            out[level] = picked[pl.ds(pl.multiple_of(row, piece), piece), :]


def prepare(here, select, eigvecs, cols):
    local, wide = eigvecs.shape
    width = select.shape[0]
    deep, piece = cols // 2, local // cols
    in_vmem = pl.BlockSpec(memory_space=pltpu.VMEM)
    some = jax.ShapeDtypeStruct((deep, piece, width), BF16)
    return pl.pallas_call(
        prepare_kernel,
        out_shape=(some, some),
        in_specs=[pl.BlockSpec(memory_space=pltpu.SMEM), in_vmem, in_vmem],
        out_specs=(in_vmem,) * 2,
        scratch_shapes=[pltpu.VMEM((local, width), BF16)],
        compiler_params=pltpu.CompilerParams(vmem_limit_bytes=16 << 20),
        cost_estimate=pl.CostEstimate(
            flops=2 * local * wide * width, bytes_accessed=4 * local * wide, transcendentals=0
        ),
    )(here, select[None, :], eigvecs)


def halves(x):
    high = x.astype(BF16)
    return high, (x - high.astype(F32)).astype(BF16)


def moved(order, x, dims):
    width = x.shape[1]
    both = lax.dot_general(order, jnp.concatenate(halves(x), axis=1), (dims, ((), ())), preferred_element_type=F32)
    return both[:, :width] + both[:, width:]


def moved_sides(x, order, dims):
    depth = x.shape[0]
    both = lax.dot_general(jnp.concatenate(halves(x), axis=0), order, (dims, ((), ())), preferred_element_type=F32)
    return both[:depth] + both[depth:]


def close(left, right):
    left_high, left_low = halves(left)
    right_high, right_low = halves(right)
    return jnp.dot(
        jnp.concatenate([left_high, left_low, left_high], axis=1),
        jnp.concatenate([right_high, right_high, right_low], axis=0),
        preferred_element_type=F32,
    )


def factor_kernel(count, place_ref, *refs):
    mine, sib, out_ref = refs[:count], refs[count : 2 * count], refs[2 * count]
    size = out_ref.shape[0]
    half = size // 2
    turned = (((1,), (1,)), ((), ()))
    gram = jnp.zeros((size, size), F32)
    for one, other, _ in pairs_of(mine, sib):
        both = jnp.concatenate([one[...], other[...]], axis=0)
        gram = gram + lax.dot_general(both, both, turned, preferred_element_type=F32)
    reflectors = lax.broadcasted_iota(jnp.int32, (size, size), 0)
    order = jnp.where(reflectors == place_ref[...], 1.0, 0.0).astype(BF16)
    gram = moved_sides(moved(order, gram, ((1,), (0,))), order, ((1,), (1,)))
    two, one = inverses([gram[:half, :half], gram[half:, half:]])
    mixed = -precise(one, precise(gram[half:, :half], two))
    factor = jnp.concatenate(
        [
            jnp.concatenate([two, jnp.zeros_like(two)], axis=1),
            jnp.concatenate([mixed, one], axis=1),
        ],
        axis=0,
    )
    out_ref[...] = moved_sides(moved(order, factor, ((0,), (0,))), order, ((1,), (0,)))


def factor_of(place, mine, sib):
    _, half, local = mine[0].shape
    size = 2 * half
    rows = sum(part.shape[0] for part in mine)
    return pl.pallas_call(
        functools.partial(factor_kernel, len(mine)),
        out_shape=jax.ShapeDtypeStruct((size, size), F32),
        compiler_params=pltpu.CompilerParams(vmem_limit_bytes=16 << 20),
        cost_estimate=pl.CostEstimate(
            flops=2 * size * size * rows * local + 2 * 6 * 16 * size**3,
            bytes_accessed=8 * size * size + 2 * size * rows * local,
            transcendentals=0,
        ),
    )(place, *mine, *sib)


def spread_kernel(count, here_ref, map_ref, ritz_ref, *refs):
    mine, sib = refs[:count], refs[count : 2 * count]
    vec, out_ref = refs[2 * count :]
    _, half, local = mine[0].shape
    for one, other, numbers in pairs_of(mine, sib):
        start = (here_ref[0] ^ jnp.where(here_ref[2] == 0, *numbers)) * local
        for at in range(0, local, TILE):
            goal = pl.multiple_of(map_ref[(start + at) // TILE] * TILE, TILE)
            vec[:half, pl.ds(goal, TILE)] = one[:, at : at + TILE]
            vec[half:, pl.ds(goal, TILE)] = other[:, at : at + TILE]
    out_ref[...] = lax.dot_general(
        ritz_ref[...], vec[...], (((1,), (1,)), ((), ())), preferred_element_type=F32
    ).astype(BF16)


def spread(here, tile_map, ritz_basis, mine, sib):
    dofs, order = ritz_basis.shape
    size = 2 * mine[0].shape[1]
    in_vmem = pl.BlockSpec(memory_space=pltpu.VMEM)
    in_smem = pl.BlockSpec(memory_space=pltpu.SMEM)
    return pl.pallas_call(
        functools.partial(spread_kernel, len(mine)),
        out_shape=(jax.ShapeDtypeStruct((size, order), BF16), jax.ShapeDtypeStruct((dofs, size), BF16)),
        in_specs=[in_smem, in_smem] + [in_vmem] * (1 + 2 * len(mine)),
        out_specs=(in_vmem, in_vmem),
        compiler_params=pltpu.CompilerParams(vmem_limit_bytes=16 << 20),
        cost_estimate=pl.CostEstimate(
            flops=2 * order * size * dofs, bytes_accessed=2 * dofs * order, transcendentals=0
        ),
    )(here, tile_map, ritz_basis, *mine, *sib)


def modes_kernel(count, here_ref, map_ref, ritz_ref, vec_ref, spread_ref, factor_ref, *refs):
    mine, sib = refs[:count], refs[count : 2 * count]
    out_ref, sel = refs[2 * count :]
    _, deep, piece, _ = mine[0].shape
    local = 2 * deep * piece
    for one, other, numbers in pairs_of(mine, sib):
        start = (here_ref[0] ^ jnp.where(here_ref[2] == 0, *numbers)) * local
        for core, source in ((here_ref[2], one), (1 - here_ref[2], other)):
            for level in range(deep):
                row = start + ((here_ref[1] ^ level) * 2 + core) * piece
                goal = pl.multiple_of(map_ref[row // TILE] * TILE + row % TILE, piece)
                sel[pl.ds(goal, piece), :] = source[level]
    projected = jnp.dot(vec_ref[...], sel[...], preferred_element_type=F32)
    weights = close(factor_ref[...], projected).astype(BF16)
    modes = jnp.dot(ritz_ref[...], sel[...], preferred_element_type=F32)
    modes = modes - jnp.dot(spread_ref[...], weights, preferred_element_type=F32)
    out_ref[...] = modes.astype(BF16)


def modes_of(here, tile_map, ritz_basis, vec, spreads, factor, mine, sib):
    dofs, order = ritz_basis.shape
    width = mine[0].shape[-1]
    size = factor.shape[0]
    in_vmem = pl.BlockSpec(memory_space=pltpu.VMEM)
    in_smem = pl.BlockSpec(memory_space=pltpu.SMEM)
    return pl.pallas_call(
        functools.partial(modes_kernel, len(mine)),
        out_shape=jax.ShapeDtypeStruct((dofs, width), BF16),
        in_specs=[in_smem, in_smem] + [in_vmem] * (4 + 2 * len(mine)),
        out_specs=in_vmem,
        scratch_shapes=[pltpu.VMEM((order, width), BF16)],
        compiler_params=pltpu.CompilerParams(vmem_limit_bytes=16 << 20),
        cost_estimate=pl.CostEstimate(
            flops=2 * order * width * (dofs + size), bytes_accessed=2 * dofs * order, transcendentals=0
        ),
    )(here, tile_map, ritz_basis, vec, spreads, factor, *mine, *sib)


def sort_kernel(count, here_ref, map_ref, ritz_ref, *refs):
    mine, sib = refs[:count], refs[count : 2 * count]
    ritz_out, vec, out_ref = refs[2 * count :]
    _, half, local = mine[0].shape
    deep = local // TILE // 2
    blocks = list(pairs_of(mine, sib))
    rows = len(blocks)
    for one, other, numbers in blocks:
        row = here_ref[0] ^ jnp.where(here_ref[2] == 0, *numbers)
        for level in range(deep):
            for side in (0, 1):
                core = here_ref[2] ^ side
                tile = (here_ref[1] ^ level) * 2 + core
                place = ((side * rows + numbers[side]) * deep + level) * TILE
                to = slice(place, place + TILE)
                goal = pl.multiple_of(map_ref[row * 2 * deep + tile] * TILE, TILE)
                at = pl.multiple_of(tile * TILE, TILE)
                ritz_out[:, to] = ritz_ref[:, pl.ds(goal, TILE)]
                vec[:half, to] = one[:, pl.ds(at, TILE)]
                vec[half:, to] = other[:, pl.ds(at, TILE)]
    out_ref[...] = lax.dot_general(
        ritz_out[...], vec[...], (((1,), (1,)), ((), ())), preferred_element_type=F32
    ).astype(BF16)


def sort(here, tile_map, ritz_basis, mine, sib):
    dofs, order = ritz_basis.shape
    size = 2 * mine[0].shape[1]
    in_vmem = pl.BlockSpec(memory_space=pltpu.VMEM)
    in_smem = pl.BlockSpec(memory_space=pltpu.SMEM)
    return pl.pallas_call(
        functools.partial(sort_kernel, len(mine)),
        out_shape=(
            jax.ShapeDtypeStruct((dofs, order), BF16),
            jax.ShapeDtypeStruct((size, order), BF16),
            jax.ShapeDtypeStruct((dofs, size), BF16),
        ),
        in_specs=[in_smem, in_smem] + [in_vmem] * (1 + 2 * len(mine)),
        out_specs=(in_vmem,) * 3,
        compiler_params=pltpu.CompilerParams(vmem_limit_bytes=24 << 20),
        cost_estimate=pl.CostEstimate(
            flops=2 * order * size * dofs, bytes_accessed=4 * dofs * order, transcendentals=0
        ),
    )(here, tile_map, ritz_basis, *mine, *sib)


def blocks_in(parts):
    return jnp.concatenate([part[...].reshape(-1, part.shape[-1]) for part in parts], axis=0)


def first_kernel(ritz_ref, vec_ref, *refs):
    mine, (modes_ref, projected_ref) = refs[:-2], refs[-2:]
    sel = blocks_in(mine)
    depth = sel.shape[0]
    projected_ref[...] = jnp.dot(vec_ref[:, :depth], sel, preferred_element_type=F32)
    modes_ref[...] = jnp.dot(ritz_ref[:, :depth], sel, preferred_element_type=F32)


def second_kernel(ritz_ref, vec_ref, spread_ref, factor_ref, modes_ref, projected_ref, *refs):
    sib, out_ref = refs[:-1], refs[-1]
    sel = blocks_in(sib)
    depth = sel.shape[0]
    projected = projected_ref[...] + jnp.dot(vec_ref[:, depth:], sel, preferred_element_type=F32)
    weights = close(factor_ref[...], projected).astype(BF16)
    modes = modes_ref[...] + jnp.dot(ritz_ref[:, depth:], sel, preferred_element_type=F32)
    modes = modes - jnp.dot(spread_ref[...], weights, preferred_element_type=F32)
    out_ref[...] = modes.astype(BF16)


def modes_in_two(ritz_sorted, vec, spreads, factor, mine, sib):
    dofs, order = ritz_sorted.shape
    width = mine[0].shape[-1]
    size = factor.shape[0]
    in_vmem = pl.BlockSpec(memory_space=pltpu.VMEM)
    params = pltpu.CompilerParams(vmem_limit_bytes=16 << 20)
    cost = pl.CostEstimate(
        flops=order * width * (dofs + size), bytes_accessed=dofs * order, transcendentals=0
    )
    modes, projected = pl.pallas_call(
        first_kernel,
        out_shape=(jax.ShapeDtypeStruct((dofs, width), F32), jax.ShapeDtypeStruct((size, width), F32)),
        in_specs=[in_vmem] * (2 + len(mine)),
        out_specs=(in_vmem, in_vmem),
        compiler_params=params,
        cost_estimate=cost,
    )(ritz_sorted, vec, *mine)
    return pl.pallas_call(
        second_kernel,
        out_shape=jax.ShapeDtypeStruct((dofs, width), BF16),
        in_specs=[in_vmem] * (6 + len(sib)),
        out_specs=in_vmem,
        compiler_params=params,
        cost_estimate=cost,
    )(ritz_sorted, vec, spreads, factor, modes, projected, *sib)


def per_device(rows, cols, eigvecs, house_one, house_two, tile_map, select, ritz_basis):
    deep = cols // 2
    row_at, col_at = lax.axis_index("row"), lax.axis_index("col")
    deep_at, core_at = col_at // 2, col_at % 2
    here = jnp.stack([row_at, deep_at, core_at]).astype(jnp.int32)
    local, wide = eigvecs.shape
    share = house_one.shape[1]
    size = 2 * share * cols

    def to_core(x):
        return lax.ppermute(x, "col", [(i, i ^ 1) for i in range(cols)])

    def to_deep(x, level):
        return lax.ppermute(x, "col", [(i, i ^ (2 * level)) for i in range(cols)])

    def to_row(x, peer):
        return lax.ppermute(x, "row", [(i, i ^ peer) for i in range(rows)])

    steps = rows.bit_length() - 1

    def over_step(x, step):
        pairs = []
        for row in range(rows):
            for col in range(cols):
                bit = steps - 1 - step if col % 2 else step
                pairs.append((row * cols + col, (row ^ (1 << bit)) * cols + col))
        return lax.ppermute(x, ("row", "col"), pairs)

    def over_rows(x, after=None):
        parts = [x[None]]
        for step in range(steps):
            held = jnp.concatenate(parts) if step else parts[0]
            if after is not None:
                held = lax.optimization_barrier((held, after(step)))[0]
            parts.append(over_step(held, step))
        return parts

    keep, give = prepare(here, select, eigvecs, cols)
    own = jnp.pad(house_two.T, ((0, share), (0, 0))) + jnp.pad(house_one.T, ((share, 0), (0, 0)))
    own = own.astype(BF16)

    got, own = lax.optimization_barrier((to_core(give), own))
    keep = keep + got

    mine_here = jnp.concatenate([own] + [to_deep(own, level) for level in range(1, deep)], axis=0)
    mine_here, keep = lax.optimization_barrier((mine_here, keep))
    mine_v = over_rows(mine_here)
    sib_v = [to_core(x) for x in mine_v]

    part = wide // rows
    here_v = jnp.concatenate([mine_here, sib_v[0][0]], axis=0)
    partial = jnp.dot(here_v, eigvecs.astype(BF16), preferred_element_type=F32)

    def chunk_of(number):
        away = jnp.where(core_at == 0, number, mirrored(number, rows))
        return lax.dynamic_slice_in_dim(partial, (row_at ^ away) * part, part, axis=1)

    chunks = jnp.stack([chunk_of(number) for number in range(rows)])
    block, chunks = lax.optimization_barrier((keep[0], chunks))
    sums = []
    for step in reversed(range(steps)):
        kept = 1 << step
        chunks = chunks[:kept] + over_step(chunks[kept:].astype(BF16), step).astype(F32)
        sums.append(chunks)
    projected = chunks[0]

    arrival = jnp.arange(size, dtype=jnp.int32)
    at_share = arrival % share
    at_block = arrival // share % 2
    at_level = arrival // (2 * share) % deep
    at_core = arrival // (2 * share * deep)
    place = at_block * (size // 2) + ((at_level ^ deep_at) * 2 + (at_core ^ core_at)) * share + at_share
    factor = factor_of(place[None, :], mine_v, sib_v)

    for level in range(1, deep):
        block = block + to_deep(keep[level], level)
    mine_sel = jnp.stack([block] + [to_deep(block, level) for level in range(1, deep)])
    mine_e = over_rows(mine_sel, lambda step: sums[step] if step else (sums[step], sib_v))
    sib_e = [to_core(x) for x in mine_e]

    weights = precise(factor, projected).astype(BF16)
    all_weights = jnp.zeros((size, wide), BF16)
    for peer in range(rows):
        arrived = to_row(weights, peer) if peer else weights
        all_weights = lax.dynamic_update_slice_in_dim(all_weights, arrived, (row_at ^ peer) * part, axis=1)
    change = lax.dot_general(here_v, all_weights, (((0,), (0,)), ((), ())), preferred_element_type=F32)
    back_vectors = eigvecs - change

    if local // cols == TILE:
        ritz_sorted, vec, spreads = sort(here, tile_map, ritz_basis, mine_v, sib_v)
        modes = modes_in_two(ritz_sorted, vec, spreads, factor, mine_e, sib_e)
    else:
        vec, spreads = spread(here, tile_map, ritz_basis, mine_v, sib_v)
        modes = modes_of(here, tile_map, ritz_basis, vec, spreads, factor, mine_e, sib_e)
    return back_vectors, modes


def solution(mesh):
    return jax.shard_map(
        functools.partial(per_device, mesh.shape["row"], mesh.shape["col"]),
        mesh=mesh,
        in_specs=(P("row", "col"), P("row", "col"), P("row", "col"), P(), P(), P(("row", "col"), None)),
        out_specs=(P("row", "col"), P(("row", "col"), None)),
        check_vma=False,
    )
```

```python
import functools

import jax
import jax.numpy as jnp
from jax import lax
from jax.experimental import pallas as pl
from jax.experimental.pallas import tpu as pltpu
from jax.sharding import PartitionSpec as P

TILE = 128
F32 = jnp.float32
BF16 = jnp.bfloat16


def precise(left, right):
    return jnp.dot(left, right, precision=lax.Precision.HIGHEST, preferred_element_type=F32)


def inverses(grams):
    width = grams[0].shape[0]
    rows = lax.broadcasted_iota(jnp.int32, (width, width), 0)
    cols = lax.broadcasted_iota(jnp.int32, (width, width), 1)
    identity = (rows == cols).astype(F32)
    powers, totals, downs = [], [], []
    for gram in grams:
        diagonal = 0.5 * gram * identity
        across = 1.0 / jnp.sum(diagonal, axis=1, keepdims=True)
        downs.append(1.0 / jnp.sum(diagonal, axis=0, keepdims=True))
        power = jnp.where(rows < cols, -gram * across, 0.0)
        powers.append(power)
        totals.append(identity + power)
    for _ in range((width - 1).bit_length() - 1):
        powers = [precise(power, power) for power in powers]
        totals = [precise(total, identity + power) for total, power in zip(totals, powers)]
    return [total * down for total, down in zip(totals, downs)]


def mirrored(number, rows):
    bits = rows.bit_length() - 1
    return sum(1 << (bits - 1 - bit) for bit in range(bits) if number >> bit & 1)


def pairs_of(mine, sib):
    mine = [part.at[at] for part in mine for at in range(part.shape[0])]
    sib = [part.at[at] for part in sib for at in range(part.shape[0])]
    rows = len(mine)
    for number in range(rows):
        other = mirrored(number, rows)
        yield mine[number], sib[other], (number, other)


def prepare_kernel(here_ref, select_ref, eig_ref, keep_ref, give_ref, picked):
    deep_at, core_at = here_ref[1], here_ref[2]
    local, wide = eig_ref.shape
    deep, piece, width = keep_ref.shape
    ids = lax.broadcasted_iota(jnp.int32, (wide, width), 0) + (deep_at * 2 + core_at) * wide
    chooser = jnp.where(ids == select_ref[...], 1.0, 0.0).astype(BF16)
    picked[...] = jnp.dot(eig_ref[...].astype(BF16), chooser, preferred_element_type=F32).astype(BF16)
    for level in range(deep):
        for out, core in ((keep_ref, core_at), (give_ref, 1 - core_at)):
            row = ((deep_at ^ level) * 2 + core) * piece
            out[level] = picked[pl.ds(pl.multiple_of(row, piece), piece), :]


def prepare(here, select, eigvecs, cols):
    local, wide = eigvecs.shape
    width = select.shape[0]
    deep, piece = cols // 2, local // cols
    in_vmem = pl.BlockSpec(memory_space=pltpu.VMEM)
    some = jax.ShapeDtypeStruct((deep, piece, width), BF16)
    return pl.pallas_call(
        prepare_kernel,
        out_shape=(some, some),
        in_specs=[pl.BlockSpec(memory_space=pltpu.SMEM), in_vmem, in_vmem],
        out_specs=(in_vmem,) * 2,
        scratch_shapes=[pltpu.VMEM((local, width), BF16)],
        compiler_params=pltpu.CompilerParams(vmem_limit_bytes=16 << 20),
        cost_estimate=pl.CostEstimate(
            flops=2 * local * wide * width, bytes_accessed=4 * local * wide, transcendentals=0
        ),
    )(here, select[None, :], eigvecs)


def halves(x):
    high = x.astype(BF16)
    return high, (x - high.astype(F32)).astype(BF16)


def moved(order, x, dims):
    width = x.shape[1]
    both = lax.dot_general(order, jnp.concatenate(halves(x), axis=1), (dims, ((), ())), preferred_element_type=F32)
    return both[:, :width] + both[:, width:]


def moved_sides(x, order, dims):
    depth = x.shape[0]
    both = lax.dot_general(jnp.concatenate(halves(x), axis=0), order, (dims, ((), ())), preferred_element_type=F32)
    return both[:depth] + both[depth:]


def close(left, right):
    left_high, left_low = halves(left)
    right_high, right_low = halves(right)
    return jnp.dot(
        jnp.concatenate([left_high, left_low, left_high], axis=1),
        jnp.concatenate([right_high, right_high, right_low], axis=0),
        preferred_element_type=F32,
    )


def factor_kernel(count, place_ref, *refs):
    mine, sib, out_ref = refs[:count], refs[count : 2 * count], refs[2 * count]
    size = out_ref.shape[0]
    half = size // 2
    turned = (((1,), (1,)), ((), ()))
    gram = jnp.zeros((size, size), F32)
    for one, other, _ in pairs_of(mine, sib):
        both = jnp.concatenate([one[...], other[...]], axis=0)
        gram = gram + lax.dot_general(both, both, turned, preferred_element_type=F32)
    reflectors = lax.broadcasted_iota(jnp.int32, (size, size), 0)
    order = jnp.where(reflectors == place_ref[...], 1.0, 0.0).astype(BF16)
    gram = moved_sides(moved(order, gram, ((1,), (0,))), order, ((1,), (1,)))
    two, one = inverses([gram[:half, :half], gram[half:, half:]])
    mixed = -precise(one, precise(gram[half:, :half], two))
    factor = jnp.concatenate(
        [
            jnp.concatenate([two, jnp.zeros_like(two)], axis=1),
            jnp.concatenate([mixed, one], axis=1),
        ],
        axis=0,
    )
    out_ref[...] = moved_sides(moved(order, factor, ((0,), (0,))), order, ((1,), (0,)))


def factor_of(place, mine, sib):
    _, half, local = mine[0].shape
    size = 2 * half
    rows = sum(part.shape[0] for part in mine)
    return pl.pallas_call(
        functools.partial(factor_kernel, len(mine)),
        out_shape=jax.ShapeDtypeStruct((size, size), F32),
        compiler_params=pltpu.CompilerParams(vmem_limit_bytes=16 << 20),
        cost_estimate=pl.CostEstimate(
            flops=2 * size * size * rows * local + 2 * 6 * 16 * size**3,
            bytes_accessed=8 * size * size + 2 * size * rows * local,
            transcendentals=0,
        ),
    )(place, *mine, *sib)


def spread_kernel(count, here_ref, map_ref, ritz_ref, *refs):
    mine, sib = refs[:count], refs[count : 2 * count]
    vec, out_ref = refs[2 * count :]
    _, half, local = mine[0].shape
    for one, other, numbers in pairs_of(mine, sib):
        start = (here_ref[0] ^ jnp.where(here_ref[2] == 0, *numbers)) * local
        for at in range(0, local, TILE):
            goal = pl.multiple_of(map_ref[(start + at) // TILE] * TILE, TILE)
            vec[:half, pl.ds(goal, TILE)] = one[:, at : at + TILE]
            vec[half:, pl.ds(goal, TILE)] = other[:, at : at + TILE]
    out_ref[...] = lax.dot_general(
        ritz_ref[...], vec[...], (((1,), (1,)), ((), ())), preferred_element_type=F32
    ).astype(BF16)


def spread(here, tile_map, ritz_basis, mine, sib):
    dofs, order = ritz_basis.shape
    size = 2 * mine[0].shape[1]
    in_vmem = pl.BlockSpec(memory_space=pltpu.VMEM)
    in_smem = pl.BlockSpec(memory_space=pltpu.SMEM)
    return pl.pallas_call(
        functools.partial(spread_kernel, len(mine)),
        out_shape=(jax.ShapeDtypeStruct((size, order), BF16), jax.ShapeDtypeStruct((dofs, size), BF16)),
        in_specs=[in_smem, in_smem] + [in_vmem] * (1 + 2 * len(mine)),
        out_specs=(in_vmem, in_vmem),
        compiler_params=pltpu.CompilerParams(vmem_limit_bytes=16 << 20),
        cost_estimate=pl.CostEstimate(
            flops=2 * order * size * dofs, bytes_accessed=2 * dofs * order, transcendentals=0
        ),
    )(here, tile_map, ritz_basis, *mine, *sib)


def modes_kernel(count, here_ref, map_ref, ritz_ref, vec_ref, spread_ref, factor_ref, *refs):
    mine, sib = refs[:count], refs[count : 2 * count]
    out_ref, sel = refs[2 * count :]
    _, deep, piece, _ = mine[0].shape
    local = 2 * deep * piece
    for one, other, numbers in pairs_of(mine, sib):
        start = (here_ref[0] ^ jnp.where(here_ref[2] == 0, *numbers)) * local
        for core, source in ((here_ref[2], one), (1 - here_ref[2], other)):
            for level in range(deep):
                row = start + ((here_ref[1] ^ level) * 2 + core) * piece
                goal = pl.multiple_of(map_ref[row // TILE] * TILE + row % TILE, piece)
                sel[pl.ds(goal, piece), :] = source[level]
    projected = jnp.dot(vec_ref[...], sel[...], preferred_element_type=F32)
    weights = close(factor_ref[...], projected).astype(BF16)
    modes = jnp.dot(ritz_ref[...], sel[...], preferred_element_type=F32)
    modes = modes - jnp.dot(spread_ref[...], weights, preferred_element_type=F32)
    out_ref[...] = modes.astype(BF16)


def modes_of(here, tile_map, ritz_basis, vec, spreads, factor, mine, sib):
    dofs, order = ritz_basis.shape
    width = mine[0].shape[-1]
    size = factor.shape[0]
    in_vmem = pl.BlockSpec(memory_space=pltpu.VMEM)
    in_smem = pl.BlockSpec(memory_space=pltpu.SMEM)
    return pl.pallas_call(
        functools.partial(modes_kernel, len(mine)),
        out_shape=jax.ShapeDtypeStruct((dofs, width), BF16),
        in_specs=[in_smem, in_smem] + [in_vmem] * (4 + 2 * len(mine)),
        out_specs=in_vmem,
        scratch_shapes=[pltpu.VMEM((order, width), BF16)],
        compiler_params=pltpu.CompilerParams(vmem_limit_bytes=16 << 20),
        cost_estimate=pl.CostEstimate(
            flops=2 * order * width * (dofs + size), bytes_accessed=2 * dofs * order, transcendentals=0
        ),
    )(here, tile_map, ritz_basis, vec, spreads, factor, *mine, *sib)


def sort_kernel(count, here_ref, map_ref, ritz_ref, *refs):
    mine, sib = refs[:count], refs[count : 2 * count]
    ritz_out, vec, out_ref = refs[2 * count :]
    _, half, local = mine[0].shape
    deep = local // TILE // 2
    blocks = list(pairs_of(mine, sib))
    rows = len(blocks)
    for one, other, numbers in blocks:
        row = here_ref[0] ^ jnp.where(here_ref[2] == 0, *numbers)
        for level in range(deep):
            for side in (0, 1):
                core = here_ref[2] ^ side
                tile = (here_ref[1] ^ level) * 2 + core
                place = ((side * rows + numbers[side]) * deep + level) * TILE
                to = slice(place, place + TILE)
                goal = pl.multiple_of(map_ref[row * 2 * deep + tile] * TILE, TILE)
                at = pl.multiple_of(tile * TILE, TILE)
                ritz_out[:, to] = ritz_ref[:, pl.ds(goal, TILE)]
                vec[:half, to] = one[:, pl.ds(at, TILE)]
                vec[half:, to] = other[:, pl.ds(at, TILE)]
    out_ref[...] = lax.dot_general(
        ritz_out[...], vec[...], (((1,), (1,)), ((), ())), preferred_element_type=F32
    ).astype(BF16)


def sort(here, tile_map, ritz_basis, mine, sib):
    dofs, order = ritz_basis.shape
    size = 2 * mine[0].shape[1]
    in_vmem = pl.BlockSpec(memory_space=pltpu.VMEM)
    in_smem = pl.BlockSpec(memory_space=pltpu.SMEM)
    return pl.pallas_call(
        functools.partial(sort_kernel, len(mine)),
        out_shape=(
            jax.ShapeDtypeStruct((dofs, order), BF16),
            jax.ShapeDtypeStruct((size, order), BF16),
            jax.ShapeDtypeStruct((dofs, size), BF16),
        ),
        in_specs=[in_smem, in_smem] + [in_vmem] * (1 + 2 * len(mine)),
        out_specs=(in_vmem,) * 3,
        compiler_params=pltpu.CompilerParams(vmem_limit_bytes=24 << 20),
        cost_estimate=pl.CostEstimate(
            flops=2 * order * size * dofs, bytes_accessed=4 * dofs * order, transcendentals=0
        ),
    )(here, tile_map, ritz_basis, *mine, *sib)


def blocks_in(parts):
    return jnp.concatenate([part[...].reshape(-1, part.shape[-1]) for part in parts], axis=0)


def first_kernel(ritz_ref, vec_ref, *refs):
    mine, (modes_ref, projected_ref) = refs[:-2], refs[-2:]
    sel = blocks_in(mine)
    depth = sel.shape[0]
    projected_ref[...] = jnp.dot(vec_ref[:, :depth], sel, preferred_element_type=F32)
    modes_ref[...] = jnp.dot(ritz_ref[:, :depth], sel, preferred_element_type=F32)


def second_kernel(ritz_ref, vec_ref, spread_ref, factor_ref, modes_ref, projected_ref, *refs):
    sib, out_ref = refs[:-1], refs[-1]
    sel = blocks_in(sib)
    depth = sel.shape[0]
    projected = projected_ref[...] + jnp.dot(vec_ref[:, depth:], sel, preferred_element_type=F32)
    weights = close(factor_ref[...], projected).astype(BF16)
    modes = modes_ref[...] + jnp.dot(ritz_ref[:, depth:], sel, preferred_element_type=F32)
    modes = modes - jnp.dot(spread_ref[...], weights, preferred_element_type=F32)
    out_ref[...] = modes.astype(BF16)


def modes_in_two(ritz_sorted, vec, spreads, factor, mine, sib):
    dofs, order = ritz_sorted.shape
    width = mine[0].shape[-1]
    size = factor.shape[0]
    in_vmem = pl.BlockSpec(memory_space=pltpu.VMEM)
    params = pltpu.CompilerParams(vmem_limit_bytes=16 << 20)
    cost = pl.CostEstimate(
        flops=order * width * (dofs + size), bytes_accessed=dofs * order, transcendentals=0
    )
    modes, projected = pl.pallas_call(
        first_kernel,
        out_shape=(jax.ShapeDtypeStruct((dofs, width), F32), jax.ShapeDtypeStruct((size, width), F32)),
        in_specs=[in_vmem] * (2 + len(mine)),
        out_specs=(in_vmem, in_vmem),
        compiler_params=params,
        cost_estimate=cost,
    )(ritz_sorted, vec, *mine)
    return pl.pallas_call(
        second_kernel,
        out_shape=jax.ShapeDtypeStruct((dofs, width), BF16),
        in_specs=[in_vmem] * (6 + len(sib)),
        out_specs=in_vmem,
        compiler_params=params,
        cost_estimate=cost,
    )(ritz_sorted, vec, spreads, factor, modes, projected, *sib)


def per_device(rows, cols, eigvecs, house_one, house_two, tile_map, select, ritz_basis):
    deep = cols // 2
    row_at, col_at = lax.axis_index("row"), lax.axis_index("col")
    deep_at, core_at = col_at // 2, col_at % 2
    here = jnp.stack([row_at, deep_at, core_at]).astype(jnp.int32)
    local, wide = eigvecs.shape
    share = house_one.shape[1]
    size = 2 * share * cols

    def to_core(x):
        return lax.ppermute(x, "col", [(i, i ^ 1) for i in range(cols)])

    def to_deep(x, level):
        return lax.ppermute(x, "col", [(i, i ^ (2 * level)) for i in range(cols)])

    def to_row(x, peer):
        return lax.ppermute(x, "row", [(i, i ^ peer) for i in range(rows)])

    steps = rows.bit_length() - 1

    def over_step(x, step):
        pairs = []
        for row in range(rows):
            for col in range(cols):
                bit = steps - 1 - step if col % 2 else step
                pairs.append((row * cols + col, (row ^ (1 << bit)) * cols + col))
        return lax.ppermute(x, ("row", "col"), pairs)

    def over_rows(x, after=None):
        parts = [x[None]]
        for step in range(steps):
            held = jnp.concatenate(parts) if step else parts[0]
            if after is not None:
                held = lax.optimization_barrier((held, after(step)))[0]
            parts.append(over_step(held, step))
        return parts

    keep, give = prepare(here, select, eigvecs, cols)
    own = jnp.pad(house_two.T, ((0, share), (0, 0))) + jnp.pad(house_one.T, ((share, 0), (0, 0)))
    own = own.astype(BF16)

    got, own = lax.optimization_barrier((to_core(give), own))
    keep = keep + got

    mine_here = jnp.concatenate([own] + [to_deep(own, level) for level in range(1, deep)], axis=0)
    mine_here, keep = lax.optimization_barrier((mine_here, keep))
    mine_v = over_rows(mine_here)
    sib_v = [to_core(x) for x in mine_v]

    part = wide // rows
    here_v = jnp.concatenate([mine_here, sib_v[0][0]], axis=0)
    partial = jnp.dot(here_v, eigvecs.astype(BF16), preferred_element_type=F32)

    def chunk_of(number):
        away = jnp.where(core_at == 0, number, mirrored(number, rows))
        return lax.dynamic_slice_in_dim(partial, (row_at ^ away) * part, part, axis=1)

    chunks = jnp.stack([chunk_of(number) for number in range(rows)])
    block = keep[0]
    sums = []
    for step in reversed(range(steps)):
        kept = 1 << step
        chunks = chunks[:kept] + over_step(chunks[kept:].astype(BF16), step).astype(F32)
        sums.append(chunks)
    projected = chunks[0]

    arrival = jnp.arange(size, dtype=jnp.int32)
    at_share = arrival % share
    at_block = arrival // share % 2
    at_level = arrival // (2 * share) % deep
    at_core = arrival // (2 * share * deep)
    place = at_block * (size // 2) + ((at_level ^ deep_at) * 2 + (at_core ^ core_at)) * share + at_share
    factor = factor_of(place[None, :], mine_v, sib_v)

    for level in range(1, deep):
        block = block + to_deep(keep[level], level)
    mine_sel = jnp.stack([block] + [to_deep(block, level) for level in range(1, deep)])
    mine_e = over_rows(mine_sel, lambda step: (sums[-1], sib_v))
    sib_e = [to_core(x) for x in mine_e]

    weights = jnp.dot(factor, projected, precision=lax.Precision.HIGH, preferred_element_type=F32).astype(BF16)
    all_weights = jnp.zeros((size, wide), BF16)
    for peer in range(rows):
        arrived = to_row(weights, peer) if peer else weights
        all_weights = lax.dynamic_update_slice_in_dim(all_weights, arrived, (row_at ^ peer) * part, axis=1)
    change = lax.dot_general(here_v, all_weights, (((0,), (0,)), ((), ())), preferred_element_type=F32)
    back_vectors = eigvecs - change

    if local // cols == TILE:
        ritz_sorted, vec, spreads = sort(here, tile_map, ritz_basis, mine_v, sib_v)
        modes = modes_in_two(ritz_sorted, vec, spreads, factor, mine_e, sib_e)
    else:
        vec, spreads = spread(here, tile_map, ritz_basis, mine_v, sib_v)
        modes = modes_of(here, tile_map, ritz_basis, vec, spreads, factor, mine_e, sib_e)
    return back_vectors, modes


def solution(mesh):
    return jax.shard_map(
        functools.partial(per_device, mesh.shape["row"], mesh.shape["col"]),
        mesh=mesh,
        in_specs=(P("row", "col"), P("row", "col"), P("row", "col"), P(), P(), P(("row", "col"), None)),
        out_specs=(P("row", "col"), P(("row", "col"), None)),
        check_vma=False,
    )
```
